128 devices in a mesh: grp: 8 (over y, z_hi), ctx: 16 (over x, z_lo, core).
Axes of the slice: x: 4, y: 4, z: 4 (z_hi: 2, z_lo: 2; z = z_hi * 2 + z_lo), core: 2. Of those that a mesh axis runs over, the one named last changes fastest.
Arguments:
- tokens: bfloat16 [16384, 2048], P(('grp', 'ctx')), may hold values from -3 to 3
- queries: bfloat16 [16384, 4096], P(('grp', 'ctx')), may hold values from -6 to 6
- keys_values: bfloat16 [8, 4096, 1024], P('grp', 'ctx'), may hold values from -600 to 600
- out_weight: bfloat16 [4096, 2048], P('grp'), may hold values from -1 to 1
- moe_gain: float32 [2048], replicated, may hold values from 0.1 to 1.9
- expert_ids: int32 [16384, 8], P(('grp', 'ctx')), may hold values from 0 to 127, all different within a row; in each aligned block of 128 rows (0 to 127, 128 to 255, ...) at most 12 rows name the same one
- gates: float32 [16384, 8], P(('grp', 'ctx')), may hold values from 0.05 to 0.3
- w_gate_experts: bfloat16 [128, 2048, 768], P(('grp', 'ctx')), may hold values from -0.125 to 0.125
- w_up_experts: bfloat16 [128, 2048, 768], P(('grp', 'ctx')), may hold values from -0.125 to 0.125
- w_down_experts: bfloat16 [128, 768, 2048], P(('grp', 'ctx')), may hold values from -0.21875 to 0.21875
Outputs:
- layer_out: bfloat16 [16384, 2048], P(('grp', 'ctx'))
The draws below stay inside these ranges and needn't reach their ends.
Inputs may be any that keep to these rules, and one draw needn't show every extreme that they name: `expert_ids`: each row names 8 different experts; among the 128 rows of one device no expert is named more than 12 times, a bound that some block reaches.
All inputs are finite; a program needn't handle non-finite values.
Results may differ from the reference program's by a relative error of at most 0.015.
Values may be sent and summed in bfloat16 or wider, within the bound.
A program may use at most 128 MiB of HBM per device.

```python
import math
import jax
import jax.numpy as jnp
import numpy as np
from jax import lax

D = 2048
H = 32
KV_HEADS = 4
HEAD_DIM = 128
FF = 768
EXPERTS = 128
TOPK = 8
TOK_DEV = 128
CAP = 12
KEYS = 4096
SEQS = 8
TOKENS = 16384


def draw_keys_values(key, part):
    width = KV_HEADS * HEAD_DIM
    first_key = jax.random.fold_in(jax.random.fold_in(key, 17), 0)
    drawn = jnp.clip(jax.random.normal(first_key, (SEQS, KEYS, 2 * width), jnp.float32), -5.0, 5.0)
    return drawn.astype(jnp.bfloat16)


def block_scale(own_key, dims, cuts, smallest, high):
    level, own = 1.0, jax.random.fold_in(own_key, 6)
    for dim, blocks in cuts:
        steps = jnp.exp(jax.random.uniform(jax.random.fold_in(own, dim), (blocks,), jnp.float32, smallest / len(cuts), high / len(cuts)))
        level = level * jnp.repeat(steps, dims[dim] // blocks).reshape([-1 if axis == dim else 1 for axis in range(len(dims))])
    return level


def routed_block(own_key, own, number, rows, amount, top, reach, skew):
    order = jax.random.permutation(own_key, amount)
    crowded, common = shares(amount, rows * top, reach, skew, True), shares(amount, rows * top, reach, skew, False)
    places = jnp.arange(amount)

    def named(lengths, rotation):
        used = int((lengths > 0).sum())
        fixed = max(1, used // 4)
        moved = fixed + (places - fixed + rotation * (used - fixed)) % max(1, amount - fixed)
        return jnp.zeros((amount,), jnp.int32).at[order[jnp.where(places < fixed, places, moved)]].set(jnp.asarray(lengths, jnp.int32))

    lengths = jnp.where(number % 4 == 0, named(crowded, number // 4), named(common, number - number // 4 - 1))
    mixed = jax.random.permutation(jax.random.fold_in(own, 3), amount)
    donor, receiver = mixed[0:amount // 2 * 2:2], mixed[1:amount // 2 * 2:2]
    margin = jnp.minimum(lengths[donor] - 1, reach - lengths[receiver]) // 2
    margin = jnp.where((donor == order[0]) | (receiver == order[0]) | (lengths[receiver] == 0), 0, jnp.maximum(margin, 0))
    moved = jax.random.randint(jax.random.fold_in(own, 4), (amount // 2,), 0, 1 << 20) % (margin + 1)
    lengths = lengths.at[donor].add(-moved).at[receiver].add(moved)
    labels = jnp.searchsorted(jnp.cumsum(lengths), jnp.arange(rows * top), side="right").astype(jnp.int32)
    table = labels.reshape(top, rows).T
    table = table[jax.random.permutation(jax.random.fold_in(own, 1), rows)]
    rotation = jax.random.randint(jax.random.fold_in(own, 2), (rows, 1), 0, top)
    return jnp.take_along_axis(table, (jnp.arange(top)[None, :] + rotation) % top, axis=1)


def shares(count, total, most, slope, full):
    weights = [(1 << 20) // math.isqrt(standing ** slope) + 1 for standing in range(1, count + 1)]
    largest = most if full else min(most, max(-(-total // count), total * weights[0] // sum(weights)))
    least = 1 if total - largest >= count - 1 else 0
    counts, spare = [largest] + [least] * (count - 1), total - largest - least * (count - 1)
    while spare > 0:
        candidates = [i for i in range(1, count) if counts[i] < largest] or [i for i in range(1, count) if counts[i] < most]
        mass, remaining = sum([weights[i] for i in candidates]), spare
        for i in candidates:
            more = min(most - counts[i], max(1, remaining * weights[i] // mass), spare)
            counts[i] = counts[i] + more
            spare = spare - more
    return np.array(counts)


def gaussian(stream_key, dims, deviation, most, pieces=(), held_as=jnp.bfloat16):
    gain = block_scale(stream_key, dims, pieces, -0.22, 0.18) if pieces else 1.0
    entries = jax.random.normal(stream_key, dims, jnp.float32) * deviation * gain
    return jnp.minimum(jnp.maximum(entries, -most), most).astype(held_as)


def setup_inputs(seed: int = 0) -> dict:
    key_of = jax.random.split(jax.random.key(seed), 11)
    tokens = gaussian(key_of[0], (TOKENS, D), 0.5, 3.0, ((0, 128),))
    queries = gaussian(key_of[1], (TOKENS, H * HEAD_DIM), 1.0, 6.0, ((0, 128),))
    keys_values = draw_keys_values(jax.random.fold_in(key_of[10], 71), 0)
    out_weight = gaussian(key_of[3], (H * HEAD_DIM, D), (H * HEAD_DIM // 128) ** -0.5, 1.0, ((0, 8),))
    moe_gain = jnp.clip(1.0 + 0.18 * jax.random.normal(key_of[4], (D,), jnp.float32), 0.1, 1.9)
    expert_ids_keys = jax.random.split(jax.random.fold_in(key_of[5], 1), TOKENS // TOK_DEV)
    expert_ids_turns = jax.random.permutation(jax.random.fold_in(key_of[5], 3), TOKENS // TOK_DEV)
    expert_ids = jax.vmap(lambda own, number: routed_block(jax.random.fold_in(key_of[5], 2), own, number, TOK_DEV, EXPERTS, TOPK, CAP, 2))(expert_ids_keys, expert_ids_turns).reshape((TOKENS, TOPK))
    gates = jnp.clip(0.05 + 0.25 * jax.random.uniform(key_of[6], (TOKENS, TOPK), jnp.float32) ** block_scale(key_of[6], (TOKENS, TOPK), ((0, 128),), -0.2, 0.2), 0.05, 0.3)
    w_gate_experts = gaussian(key_of[7], (EXPERTS, D, FF), D ** -0.5, 0.125, ((0, 128),))
    w_up_experts = gaussian(key_of[8], (EXPERTS, D, FF), D ** -0.5, 0.125, ((0, 128),))
    w_down_experts = gaussian(key_of[9], (EXPERTS, FF, D), FF ** -0.5, 0.21875, ((0, 128),))
    return dict(tokens=tokens, queries=queries, keys_values=keys_values, out_weight=out_weight, moe_gain=moe_gain, expert_ids=expert_ids, gates=gates, w_gate_experts=w_gate_experts, w_up_experts=w_up_experts, w_down_experts=w_down_experts)


masked_score = -1e+30

def sequence_attention(query_seq, kv_seq):
    new_count = query_seq.shape[0]
    key_count = kv_seq.shape[0]
    width = KV_HEADS * HEAD_DIM
    group_heads = H // KV_HEADS
    scaling = 1.0 / math.sqrt(HEAD_DIM)
    query_position = key_count - new_count + jnp.arange(new_count, dtype=jnp.int32)
    key_position = jnp.arange(key_count, dtype=jnp.int32)
    allowed = jnp.tile(key_position[None, :] <= query_position[:, None], (group_heads, 1))
    key_heads = kv_seq[:, :width].reshape(key_count, KV_HEADS, HEAD_DIM).transpose(1, 0, 2)
    value_heads = kv_seq[:, width:].reshape(key_count, KV_HEADS, HEAD_DIM).transpose(1, 0, 2)
    query_heads = query_seq.reshape(new_count, KV_HEADS, group_heads, HEAD_DIM).transpose(1, 2, 0, 3).reshape(KV_HEADS, group_heads * new_count, HEAD_DIM)

    def one_head(inputs):
        query_rows, key_rows, value_rows = inputs
        scores = jnp.dot(query_rows, key_rows.T, preferred_element_type=jnp.float32) * scaling
        scores = jnp.where(allowed, scores, masked_score)
        top_score = lax.optimization_barrier(jnp.max(scores, axis=1, keepdims=True))
        weights = jnp.where(allowed, jnp.exp(scores - top_score), 0.0).astype(jnp.bfloat16)
        total = lax.optimization_barrier(jnp.sum(weights.astype(jnp.float32), axis=1, keepdims=True))
        return jnp.dot(weights, value_rows, preferred_element_type=jnp.float32) / total
    outputs = lax.map(one_head, (query_heads, key_heads, value_heads))
    return outputs.reshape(KV_HEADS, group_heads, new_count, HEAD_DIM).transpose(2, 0, 1, 3).reshape(new_count, H * HEAD_DIM).astype(jnp.bfloat16)

def run_sequence(inputs):
    return sequence_attention(inputs[0], inputs[1])

def reference(tokens, queries, keys_values, out_weight, moe_gain, expert_ids, gates, w_gate_experts, w_up_experts, w_down_experts):
    query_seqs = queries.reshape(SEQS, TOKENS // SEQS, H * HEAD_DIM)
    attended = lax.map(run_sequence, (query_seqs, keys_values)).reshape(TOKENS, H * HEAD_DIM)
    projected = jnp.dot(attended, out_weight, preferred_element_type=jnp.float32)
    residual = (tokens.astype(jnp.float32) + projected).astype(jnp.bfloat16)
    wide = residual.astype(jnp.float32)
    normed = (wide * lax.rsqrt(lax.optimization_barrier(jnp.mean(wide * wide, axis=1, keepdims=True)) + 1e-06) * moe_gain).astype(jnp.bfloat16)
    block_count = TOKENS // TOK_DEV
    assigned = expert_ids.reshape(block_count, TOK_DEV * TOPK)
    one_hot = (assigned[:, :, None] == jnp.arange(EXPERTS, dtype=jnp.int32)[None, None, :]).astype(jnp.int32)
    earlier = jnp.cumsum(one_hot, axis=1) - one_hot
    slot_index = lax.optimization_barrier(jnp.sum(earlier * one_hot, axis=2))
    block_index = jnp.arange(block_count, dtype=jnp.int32)[:, None]
    position = (assigned * (block_count * CAP) + block_index * CAP + slot_index).reshape(-1).astype(jnp.int32)
    token_index = jnp.arange(TOKENS * TOPK, dtype=jnp.int32) // TOPK
    table = jnp.full((EXPERTS * block_count * CAP,), TOKENS, jnp.int32).at[position].set(token_index).reshape(EXPERTS, block_count * CAP)

    def run_expert(inputs):
        table_row, gate_matrix, up_matrix, down_matrix = inputs
        present = table_row < TOKENS
        gathered = jnp.where(present[:, None], normed[jnp.minimum(table_row, TOKENS - 1)], 0.0).astype(jnp.bfloat16)
        gate_part = jnp.dot(gathered, gate_matrix, preferred_element_type=jnp.float32)
        up_part = jnp.dot(gathered, up_matrix, preferred_element_type=jnp.float32)
        hidden = (jax.nn.silu(gate_part) * up_part).astype(jnp.bfloat16)
        return jnp.dot(hidden, down_matrix, preferred_element_type=jnp.float32).astype(jnp.bfloat16)
    expert_outputs = lax.map(run_expert, (table, w_gate_experts, w_up_experts, w_down_experts))
    picked = expert_outputs.reshape(EXPERTS * block_count * CAP, D)[position].reshape(TOKENS, TOPK, D)
    combined = lax.optimization_barrier(jnp.sum(picked.astype(jnp.float32) * gates[:, :, None], axis=1))
    return (residual.astype(jnp.float32) + combined).astype(jnp.bfloat16)
```

```python
import functools
import math

import jax
import jax.numpy as jnp
from jax import lax
from jax.experimental import pallas as pl
from jax.experimental.pallas import tpu as pltpu
from jax.sharding import PartitionSpec as P

H = 32
KV_HEADS = 4
HEAD_DIM = 128
EXPERTS = 128
TOPK = 8
CAP = 12
D = 2048
TOK = 128
PAIR = 2 * CAP
CHIPS = 64
SLOTS = CHIPS * PAIR
MESH = pl.DeviceIdType.MESH
BF16 = jnp.bfloat16
F32 = jnp.float32


def place():
    g = lax.axis_index("grp")
    c = lax.axis_index("ctx")
    return g, c


def attn_kernel(
    tok_hbm, q_hbm, kv_hbm, w_hbm, gain_ref, ids_ref, gat_ref,
    resid_ref, normed_ref, p_ref, chi_ref, clo_ref,
    kvbuf, qbuf, tokbuf, idsbuf, gatbuf, wbuf, acc, mx, attn, part, sendb, recvb, tmp, valb, gb,
    kv_ssem, kv_rsem, w_ssem, w_rsem, ex_ssem, ex_rsem, pr_ssem, pr_rsem,
):
    g, c = place()
    y, hi = g // 2, g % 2
    x, z, k = c // 4, (c // 2) % 2, c % 2
    j = c // 2

    def dev(xx, zz, kk):
        return (g, ((xx % 4) * 2 + zz) * 2 + kk)

    def wdev(yy, hh, zz):
        return ((yy % 4) * 2 + hh, (x * 2 + zz) * 2 + k)

    def remote(src, dst, ss, rs, device):
        return pltpu.make_async_remote_copy(
            src_ref=src, dst_ref=dst, send_sem=ss, recv_sem=rs, device_id=device, device_id_type=MESH
        )

    partner = dev(x, z, 1 - k)
    up, down = (x + 1) % 4, (x + 3) % 4
    near = [partner]
    for h in range(2):
        near += [dev(up, z, h), dev(down, z, h), dev(x, 1 - z, h)]
    near += [wdev(y + 1, hi, z), wdev(y + 3, hi, z), wdev(y, 1 - hi, 1 - z)]
    barrier = pltpu.get_barrier_semaphore()
    for target in near:
        pl.semaphore_signal(barrier, inc=1, device_id=target, device_id_type=MESH)
    pl.semaphore_wait(barrier, len(near))

    def kv_part(h, kv):
        return kv_hbm.at[0, :, pl.ds(pl.multiple_of(kv * 512 + h * 256, 256), 256)]

    def q_part(h):
        return q_hbm.at[:, pl.ds(pl.multiple_of(h * 2048, 2048), 2048)]

    sends = []

    def push(copy):
        copy.start()
        sends.append(copy)

    locals_ = []

    def pull(copy):
        copy.start()
        locals_.append(copy)

    push(remote(q_part(1 - k), qbuf.at[k], ex_ssem.at[0], ex_rsem.at[0], partner))
    pull(pltpu.make_async_copy(q_part(k), qbuf.at[k], ex_ssem.at[4]))
    for kv in range(2):
        push(remote(kv_part(1 - k, kv), kvbuf.at[j, k, kv], kv_ssem.at[kv], kv_rsem.at[j], partner))
        pltpu.make_async_copy(kv_part(k, kv), kvbuf.at[j, k, kv], kv_rsem.at[j]).start()
    n = 2
    for target in ((up, z), (down, z), (x, 1 - z)):
        for h in range(2):
            for kv in range(2):
                push(remote(kv_part(h, kv), kvbuf.at[j, k, kv], kv_ssem.at[n], kv_rsem.at[j], dev(*target, h)))
                n += 1

    mine = y // 2 == k
    slot_own = (y % 2) * 2 + hi
    slot_own_z = (y % 2) * 2 + 1 - hi
    slot_dn = ((y + 3) % 2) * 2 + hi
    slot_up_z = ((y + 1) % 2) * 2 + 1 - hi
    down_in = ((y + 3) % 4) // 2 == k
    up_in = ((y + 1) % 4) // 2 == k

    def w_copy(src, slot, index, target):
        return remote(src, wbuf.at[slot], w_ssem.at[index], w_rsem.at[slot], target)

    own_sends = [
        w_copy(w_hbm, slot_own, 0, wdev(y, 1 - hi, 1 - z)),
        w_copy(w_hbm, slot_own, 1, wdev(y + 1, hi, z)),
        w_copy(w_hbm, slot_own, 2, wdev(y + 3, hi, z)),
    ]
    z_sends = [
        w_copy(wbuf.at[slot_own_z], slot_own_z, 3, wdev(y + 1, hi, z)),
        w_copy(wbuf.at[slot_own_z], slot_own_z, 4, wdev(y + 3, hi, z)),
    ]
    dn_send = w_copy(wbuf.at[slot_dn], slot_dn, 5, wdev(y + 1, hi, z))
    up_send = w_copy(wbuf.at[slot_up_z], slot_up_z, 6, wdev(y + 3, hi, z))

    def w_arrived(slot):
        return w_copy(wbuf.at[slot], slot, 0, partner)

    @pl.when(mine)
    def _():
        for copy in own_sends:
            copy.start()
        pltpu.make_async_copy(w_hbm, wbuf.at[slot_own], w_rsem.at[slot_own]).start()

    push(remote(tok_hbm, tokbuf.at[k], ex_ssem.at[1], ex_rsem.at[1], partner))
    pull(pltpu.make_async_copy(tok_hbm, tokbuf.at[k], ex_ssem.at[5]))
    push(remote(ids_ref, idsbuf.at[k], ex_ssem.at[2], ex_rsem.at[2], partner))
    pull(pltpu.make_async_copy(ids_ref, idsbuf.at[k], ex_ssem.at[6]))
    push(remote(gat_ref, gatbuf.at[k], ex_ssem.at[3], ex_rsem.at[3], partner))
    pull(pltpu.make_async_copy(gat_ref, gatbuf.at[k], ex_ssem.at[7]))

    acc[...] = jnp.zeros_like(acc)
    mx[...] = jnp.full_like(mx, -1e30)

    sends[0].wait_recv()
    locals_[0].wait()

    factor = math.log2(math.e) / math.sqrt(HEAD_DIM)

    def head(h, js, masked):
        cols = pl.ds(pl.multiple_of(h * 128, 128), 128)
        kvcols = pl.ds(pl.multiple_of((h // 8) * 128, 128), 128)
        q = qbuf[:, :, cols].reshape(256, 128)
        key = kvbuf[js, :, 0, :, kvcols].reshape(512, 128)
        value = kvbuf[js, :, 1, :, kvcols].reshape(512, 128)
        s = lax.dot_general(q, key, (((1,), (1,)), ((), ())), preferred_element_type=F32)
        if masked:
            row = lax.broadcasted_iota(jnp.int32, s.shape, 0) + 256 * (j % 2)
            col = lax.broadcasted_iota(jnp.int32, s.shape, 1)
            s = jnp.where(col <= row, s, -1e30)
        old = mx[h]
        new = jnp.maximum(old, jnp.max(s, axis=1, keepdims=True))
        mx[h] = new
        scale = jnp.exp2((old - new) * factor)
        wide = jnp.concatenate([new] * 4, axis=1)
        p = jnp.exp2((s - wide) * factor).astype(BF16)
        aug = jnp.concatenate([value, jnp.ones_like(value)], axis=1)
        o = jnp.dot(p, aug, preferred_element_type=F32)
        acc[h] = acc[h] * jnp.concatenate([scale, scale], axis=1) + o

    def kv_arrived(js):
        return remote(kvbuf.at[js], kvbuf.at[js], kv_ssem.at[0], kv_rsem.at[js], partner)

    def relay(js, index, target):
        return remote(kvbuf.at[js], kvbuf.at[js], kv_ssem.at[index], kv_rsem.at[js], dev(*target, k))

    chip_z = x * 2 + 1 - z
    chip_dn = down * 2 + z
    chip_up_z = up * 2 + 1 - z
    relays = [
        relay(chip_z, 14, (up, z)),
        relay(chip_z, 15, (down, z)),
        relay(chip_dn, 16, (up, z)),
        relay(chip_up_z, 17, (down, z)),
    ]

    def step(i, carry):
        dx = jnp.where(i < 2, 0, jnp.where(i >= 6, 2, jnp.where((i == 3) | (i == 4), 1, 3)))
        dz = jnp.where((i == 1) | (i == 4) | (i == 5) | (i == 7), 1, 0)
        js = ((x + dx) % 4) * 2 + (z + dz) % 2
        kv_arrived(js).wait_recv()

        @pl.when(i == 1)
        def _():
            relays[0].start()
            relays[1].start()

        @pl.when(i == 2)
        def _():
            relays[2].start()

        @pl.when(i == 4)
        def _():
            relays[3].start()

        @pl.when(i == 5)
        def _():
            @pl.when(mine)
            def _():
                w_arrived(slot_own_z).wait_recv()
                for copy in z_sends:
                    copy.start()

            @pl.when(down_in)
            def _():
                w_arrived(slot_dn).wait_recv()
                dn_send.start()

        @pl.when(js - 4 < j // 2)
        def _():
            lax.fori_loop(0, 16, lambda h, cc: (head(h, js, False), cc)[1], 0)

        @pl.when(js - 4 == j // 2)
        def _():
            lax.fori_loop(0, 16, lambda h, cc: (head(h, js, True), cc)[1], 0)

        return carry

    lax.fori_loop(0, 8, step, 0)

    @pl.when(up_in)
    def _():
        w_arrived(slot_up_z).wait_recv()
        up_send.start()

    def finish(h, carry):
        value = acc[h]
        attn[:, pl.ds(pl.multiple_of(h * 128, 128), 128)] = (value[:, :128] / value[:, 128:]).astype(BF16)
        return carry

    lax.fori_loop(0, 16, finish, 0)

    for copy in sends[len(sends) - 3:]:
        copy.wait_recv()
    for copy in locals_[1:]:
        copy.wait()
    t_from = lax.broadcasted_iota(jnp.int32, (TOK, TOK), 0)
    t_to = lax.broadcasted_iota(jnp.int32, (TOK, TOK), 1)
    before = (t_from < t_to).astype(BF16)
    expert = 2 * lax.broadcasted_iota(jnp.int32, (CHIPS, TOK), 0) + k
    for b in range(2):
        named = jnp.zeros((CHIPS, TOK), F32)
        gate = jnp.zeros((CHIPS, TOK), F32)
        for kk in range(TOPK):
            hit = idsbuf[b, kk:kk + 1, :] == expert
            named = named + jnp.where(hit, 1.0, 0.0)
            gate = gate + jnp.where(hit, gatbuf[b, kk:kk + 1, :], 0.0)
        rank = jnp.dot(named.astype(BF16), before, preferred_element_type=F32)
        valb[:, b * TOK:(b + 1) * TOK] = named * (rank + 1.0)
        gb[:, b * TOK:(b + 1) * TOK] = gate
    u = lax.broadcasted_iota(jnp.int32, (PAIR, 256), 0)
    lane = lax.broadcasted_iota(jnp.int32, (PAIR, 256), 1)
    wanted = jnp.where(u // CAP == lane // TOK, u % CAP + 1, -1).astype(F32)

    def slot_rows(values):
        def one(ch, carry):
            rows = pl.ds(pl.multiple_of(ch * PAIR, 8), PAIR)
            match = valb[pl.ds(ch, 1), :] == wanted
            filled = gb[pl.ds(ch, 1), :] if values else 1.0
            tmp[rows, :] = jnp.where(match, filled, 0.0)
            return carry

        lax.fori_loop(0, CHIPS, one, 0)

    slot_rows(False)

    def cast(i, carry):
        rows = pl.ds(pl.multiple_of(i * 192, 192), 192)
        p_ref[rows, :] = tmp[rows, :].astype(BF16)
        return carry

    lax.fori_loop(0, 8, cast, 0)
    slot_rows(True)
    for i in range(SLOTS // 256):
        turned = tmp[i * 256:(i + 1) * 256, :].T
        top = turned.astype(BF16)
        chi_ref[:, i * 256:(i + 1) * 256] = top
        clo_ref[:, i * 256:(i + 1) * 256] = (turned - top.astype(F32)).astype(BF16)

    part[...] = jnp.zeros_like(part)
    near_par = jnp.where(mine, y % 2, 1 - y % 2)

    def slot_at(i):
        return jnp.where(i < 2, near_par, 1 - near_par) * 2 + jnp.where(i % 2 == 0, hi, 1 - hi)

    own_slot = jnp.where(mine, slot_own, -1)

    def project(i, carry):
        slot = slot_at(i)
        done_z = jnp.logical_and(mine, slot == slot_own_z)
        done_dn = jnp.logical_and(down_in, slot == slot_dn)
        done_up = jnp.logical_and(up_in, slot == slot_up_z)
        seen = jnp.logical_or(done_z, jnp.logical_or(done_dn, done_up))

        @pl.when(jnp.logical_not(seen))
        def _():
            w_arrived(slot).wait_recv()

        rows = attn[:, pl.ds(pl.multiple_of(slot * 512, 512), 512)]
        for nn in range(4):
            cols = slice(nn * 512, (nn + 1) * 512)
            part[:, cols] += jnp.dot(rows, wbuf[slot, :, cols], preferred_element_type=F32)
        return carry

    lax.fori_loop(0, 4, project, 0)
    halves = []
    for nn in range(4):
        sendb[nn] = part[:, nn * 512:(nn + 1) * 512].astype(BF16)
        copy = remote(sendb.at[nn], recvb.at[nn], pr_ssem.at[nn], pr_rsem.at[nn], partner)
        copy.start()
        halves.append(copy)
    for copy in halves:
        copy.wait_recv()

    gain = gain_ref[...]

    def normalise(i, carry):
        rows = pl.ds(pl.multiple_of(i * 32, 32), 32)
        toks = tokbuf[i // 4, pl.ds(pl.multiple_of((i % 4) * 32, 32), 32), :].astype(F32)
        other = jnp.concatenate([recvb[nn, rows, :] for nn in range(4)], axis=1).astype(F32)
        residual = (toks + part[rows, :] + other).astype(BF16)
        wide = residual.astype(F32)
        mean = jnp.mean(wide * wide, axis=1, keepdims=True)
        resid_ref[rows, :] = residual
        normed_ref[rows, :] = (wide * lax.rsqrt(mean + 1e-06) * gain).astype(BF16)
        return carry

    lax.fori_loop(0, 8, normalise, 0)

    for copy in sends:
        copy.wait_send()
    for copy in relays:
        copy.wait_send()
    for copy in halves:
        copy.wait_send()

    @pl.when(mine)
    def _():
        for copy in own_sends + z_sends:
            copy.wait_send()

    @pl.when(down_in)
    def _():
        dn_send.wait_send()

    @pl.when(up_in)
    def _():
        up_send.wait_send()


def attention(tokens, queries, keys_values, out_weight, moe_gain, expert_ids, gates):
    dma = pltpu.SemaphoreType.DMA
    anywhere = pl.BlockSpec(memory_space=pl.ANY)
    vmem = pl.BlockSpec(memory_space=pltpu.VMEM)
    return pl.pallas_call(
        attn_kernel,
        name="attend",
        out_shape=(
            jax.ShapeDtypeStruct((256, D), BF16),
            jax.ShapeDtypeStruct((256, D), BF16),
            jax.ShapeDtypeStruct((SLOTS, 256), BF16),
            jax.ShapeDtypeStruct((256, SLOTS), BF16),
            jax.ShapeDtypeStruct((256, SLOTS), BF16),
        ),
        in_specs=[anywhere] * 4 + [vmem] * 3,
        out_specs=(vmem,) * 5,
        scratch_shapes=[
            pltpu.VMEM((8, 2, 2, 256, 256), BF16),
            pltpu.VMEM((2, TOK, 2048), BF16),
            pltpu.VMEM((2, TOK, D), BF16),
            pltpu.VMEM((2, TOPK, TOK), jnp.int32),
            pltpu.VMEM((2, TOPK, TOK), F32),
            pltpu.VMEM((4, 512, D), BF16),
            pltpu.VMEM((16, 256, 256), F32),
            pltpu.VMEM((16, 256, 128), F32),
            pltpu.VMEM((256, 2048), BF16),
            pltpu.VMEM((256, D), F32),
            pltpu.VMEM((4, 256, 512), BF16),
            pltpu.VMEM((4, 256, 512), BF16),
            pltpu.VMEM((SLOTS, 256), F32),
            pltpu.VMEM((CHIPS, 256), F32),
            pltpu.VMEM((CHIPS, 256), F32),
            dma((18,)), dma((8,)), dma((7,)), dma((4,)), dma((8,)), dma((4,)), dma((4,)), dma((4,)),
        ],
        compiler_params=pltpu.CompilerParams(
            collective_id=0, has_side_effects=True, vmem_limit_bytes=60 * 1024 * 1024
        ),
    )(tokens, queries, keys_values, out_weight, moe_gain.reshape(1, D), expert_ids.T, gates.T)


def per_device(
    tokens,
    queries,
    keys_values,
    out_weight,
    moe_gain,
    expert_ids,
    gates,
    w_gate_experts,
    w_up_experts,
    w_down_experts,
):
    tok_count = tokens.shape[0]
    resid2, normed2, _, _, _ = attention(
        tokens, queries, keys_values, out_weight, moe_gain, expert_ids, gates
    )
    start = (lax.axis_index("ctx") % 2) * TOK
    residual = lax.dynamic_slice_in_dim(resid2, start, TOK, 0)
    normed = lax.dynamic_slice_in_dim(normed2, start, TOK, 0)
    wide = residual.astype(jnp.float32)
    flat_ids = expert_ids.reshape(-1)
    one_hot = (flat_ids[:, None] == jnp.arange(EXPERTS, dtype=jnp.int32)[None, :]).astype(jnp.int32)
    slot_index = jnp.sum((jnp.cumsum(one_hot, axis=0) - one_hot) * one_hot, axis=1)
    position = flat_ids * CAP + slot_index
    token_index = jnp.arange(tok_count * TOPK, dtype=jnp.int32) // TOPK
    table = jnp.full((EXPERTS * CAP,), tok_count, jnp.int32).at[position].set(token_index)
    present = table < tok_count
    outgoing = jnp.where(present[:, None], normed[jnp.minimum(table, tok_count - 1)], 0.0)
    local_experts = w_gate_experts.shape[0]
    owners = EXPERTS // local_experts
    width = normed.shape[1]
    outgoing = outgoing.reshape(owners, local_experts, CAP, width)
    incoming = lax.all_to_all(outgoing, ("grp", "ctx"), split_axis=0, concat_axis=0, tiled=True)
    gate_part = jnp.einsum(
        "sjcd,jdf->sjcf", incoming, w_gate_experts, preferred_element_type=jnp.float32
    )
    up_part = jnp.einsum(
        "sjcd,jdf->sjcf", incoming, w_up_experts, preferred_element_type=jnp.float32
    )
    hidden = (jax.nn.silu(gate_part) * up_part).astype(jnp.bfloat16)
    result_rows = jnp.einsum(
        "sjcf,jfd->sjcd", hidden, w_down_experts, preferred_element_type=jnp.float32
    ).astype(jnp.bfloat16)
    returned = lax.all_to_all(result_rows, ("grp", "ctx"), split_axis=0, concat_axis=0, tiled=True)
    picked = returned.reshape(EXPERTS * CAP, width)[position].reshape(tok_count, TOPK, width)
    combined = jnp.sum(picked.astype(jnp.float32) * gates[:, :, None], axis=1)
    return (wide + combined).astype(jnp.bfloat16)


def solution(mesh):
    return jax.shard_map(
        per_device,
        mesh=mesh,
        in_specs=(
            P(("grp", "ctx"), None),
            P(("grp", "ctx"), None),
            P("grp", "ctx", None),
            P("grp", None),
            P(),
            P(("grp", "ctx"), None),
            P(("grp", "ctx"), None),
            P(("grp", "ctx"), None, None),
            P(("grp", "ctx"), None, None),
            P(("grp", "ctx"), None, None),
        ),
        out_specs=P(("grp", "ctx"), None),
        check_vma=False,
    )
```
